32 devices in a mesh: gx: 8 (over z, core), gy: 4 (over y, x).
Axes of the slice: x: 2, y: 2, z: 4, core: 2. Of those that a mesh axis runs over, the one named last changes fastest.
Arguments:
- signal: float32 [32768, 128], P(('gx', 'gy')), may hold values from -6 to 6
- filter_taps: float32 [32768, 128], P(('gx', 'gy')), may hold values from -6 to 6
- grad_out: float32 [32768, 128], P(('gx', 'gy')), may hold values from -0.03125 to 0.03125
Outputs:
- grad_signal: float32 [32768, 128], P(('gx', 'gy'))
- grad_filter: float32 [32768, 128], P(('gx', 'gy'))
The draws below stay inside these ranges and needn't reach their ends.
All inputs are finite; a program needn't handle non-finite values.
Results may differ from the reference program's by a relative error of at most 0.000098.
Values sent between devices are 32-bit elements; how exact they have to be, the bound alone decides.
A program may use at most 128 MiB of HBM per device.

```python
import jax
import jax.numpy as jnp

CH = 128
SEQ = 32768


def level_of(rng, dims, cuts, smallest, largest):
    factor_of, own = 1.0, jax.random.fold_in(rng, 6)
    for axis_at, blocks in cuts:
        heights = jnp.exp(jax.random.uniform(jax.random.fold_in(own, axis_at), (blocks,), jnp.float32, smallest / len(cuts), largest / len(cuts)))
        factor_of = factor_of * jnp.repeat(heights, dims[axis_at] // blocks).reshape([-1 if axis == axis_at else 1 for axis in range(len(dims))])
    return factor_of


def gaussian(stream_key, dims, width, bound, pieces=(), held_as=jnp.bfloat16):
    gain = level_of(stream_key, dims, pieces, -0.22, 0.18) if pieces else 1.0
    result = jax.random.normal(stream_key, dims, jnp.float32) * width * gain
    return jnp.minimum(jnp.maximum(result, -bound), bound).astype(held_as)


def setup_inputs(seed: int = 0) -> dict:
    keys = jax.random.split(jax.random.key(seed), 4)
    return {
        "signal": gaussian(keys[0], (SEQ, CH), 1.0, 6.0, ((0, 32),), jnp.float32),
        "filter_taps": gaussian(keys[1], (SEQ, CH), 1.0, 6.0, ((0, 32),), jnp.float32),
        "grad_out": gaussian(keys[2], (SEQ, CH), SEQ ** -0.5, 0.03125, ((0, 32),), jnp.float32),
    }


def reference(signal, filter_taps, grad_out):
    length = signal.shape[0]
    padded_length = 2 * length
    spec_signal = jnp.fft.fft(signal, n=padded_length, axis=0)
    spec_filter = jnp.fft.fft(filter_taps, n=padded_length, axis=0)
    spec_grad = jnp.fft.fft(grad_out, n=padded_length, axis=0)
    prod_signal = jnp.conj(spec_filter) * spec_grad
    prod_filter = jnp.conj(spec_signal) * spec_grad
    grad_signal = jnp.fft.ifft(prod_signal, axis=0)[:length].real.astype(jnp.float32)
    grad_filter = jnp.fft.ifft(prod_filter, axis=0)[:length].real.astype(jnp.float32)
    return grad_signal, grad_filter
```

```python
import math

import jax
import jax.numpy as jnp
import numpy as np
from jax import lax
from jax.experimental import pallas as pl
from jax.experimental.pallas import tpu as pltpu
from jax.sharding import PartitionSpec as P

LANES = 128
f32, bf16 = jnp.float32, jnp.bfloat16


def halves(table):
    high = table.astype(np.float32).astype(bf16)
    low = (table - high.astype(np.float64)).astype(np.float32).astype(bf16)
    return np.stack([high, low])


def make_tables(rows):
    first = 2 * rows
    period = first * LANES
    low = np.arange(rows)
    angle = 2.0 * math.pi / first * (low[:, None] * low[None, :] % first)
    outer = np.concatenate([np.cos(angle), np.sin(angle)], axis=0)
    lane = np.arange(LANES)
    angle = 2.0 * math.pi / LANES * (lane[:, None] * lane[None, :] % LANES)
    c, s = np.cos(angle), np.sin(angle)
    inner = np.concatenate(
        [np.concatenate([c, s], axis=1), np.concatenate([-s, c], axis=1)], axis=0
    )
    angle = 2.0 * math.pi / period * (np.arange(first)[:, None] * lane[None, :] % period)
    turn = np.stack([np.cos(angle), np.sin(angle)]).astype(np.float32)
    return halves(outer), halves(inner), turn


def split(value):
    high = value.astype(bf16)
    return high, (value - high.astype(f32)).astype(bf16)


def mm(a, b):
    return jnp.dot(a, b, preferred_element_type=f32)


def left_product(outer_ref, high_ref, low_ref, out_ref, width):
    total = outer_ref.shape[1]
    block = min(total, 512)

    def step(rows):
        high = high_ref[:, :width]
        low = low_ref[:, :width]
        out_ref[rows, :width] = (
            mm(outer_ref[0, rows, :], high)
            + mm(outer_ref[0, rows, :], low)
            + mm(outer_ref[1, rows, :], high)
        )

    if block == total:
        step(slice(None))
    else:

        @pl.loop(0, total // block)
        def _(i):
            step(pl.ds(pl.multiple_of(i * block, block), block))


def right_product(value, inner_ref):
    high, low = split(value)
    return mm(high, inner_ref[0]) + mm(low, inner_ref[0]) + mm(high, inner_ref[1])


def correlate(load, store, rows, outer_ref, inner_ref, turn_ref, high_ref, low_ref, prod_ref):
    odd = lax.broadcasted_iota(jnp.int32, (rows, LANES), 0) % 2 == 1
    for q in range(3):
        high, low = split(load(q))
        high32, low32 = high.astype(f32), low.astype(f32)
        at = slice(q * LANES, (q + 1) * LANES)
        high_ref[:, at], low_ref[:, at] = high, low
        at = slice((q + 3) * LANES, (q + 4) * LANES)
        high_ref[:, at] = jnp.where(odd, -high32, high32).astype(bf16)
        low_ref[:, at] = jnp.where(odd, -low32, low32).astype(bf16)
    left_product(outer_ref, high_ref, low_ref, prod_ref, 6 * LANES)
    for h in range(2):

        def part(which, q):
            at = (q + 3 * h) * LANES
            return prod_ref[which * rows : (which + 1) * rows, at : at + LANES]

        cosine = turn_ref[0, h * rows : (h + 1) * rows, :]
        sine = turn_ref[1, h * rows : (h + 1) * rows, :]

        def rotate(real, imaginary):
            return jnp.concatenate(
                [real * cosine - imaginary * sine, real * sine + imaginary * cosine], axis=1
            )

        z = rotate(part(0, 0) - part(1, 1), part(1, 0) + part(0, 1))
        g = rotate(part(0, 2), part(1, 2))
        z = right_product(z, inner_ref)
        g = right_product(g, inner_ref)
        zr, zi, gr, gi = z[:, :LANES], z[:, LANES:], g[:, :LANES], g[:, LANES:]
        y = jnp.concatenate([zr * gr + zi * gi, zi * gr - zr * gi], axis=1)
        y = right_product(y, inner_ref)
        y = rotate(y[:, :LANES], y[:, LANES:])
        high, low = split(y)
        at = slice(2 * h * LANES, 2 * (h + 1) * LANES)
        high_ref[:, at], low_ref[:, at] = high, low
    left_product(outer_ref, high_ref, low_ref, prod_ref, 4 * LANES)
    scale = 1.0 / (2 * rows * LANES)

    def part(which, q):
        return prod_ref[which * rows : (which + 1) * rows, q * LANES : (q + 1) * LANES]

    real = [part(0, 2 * h) - part(1, 2 * h + 1) for h in range(2)]
    imaginary = [part(1, 2 * h) + part(0, 2 * h + 1) for h in range(2)]
    store(0, (real[0] + jnp.where(odd, -real[1], real[1])) * scale)
    store(1, (imaginary[0] + jnp.where(odd, -imaginary[1], imaginary[1])) * scale)


def local_kernel(x_ref, outer_ref, inner_ref, turn_ref, out_ref, high_ref, low_ref, prod_ref):
    rows = x_ref.shape[2]

    @pl.loop(0, x_ref.shape[1])
    def _(c):
        def store(q, value):
            out_ref[q, c] = value

        correlate(
            lambda q: x_ref[q, c],
            store,
            rows,
            outer_ref,
            inner_ref,
            turn_ref,
            high_ref,
            low_ref,
            prod_ref,
        )


def shards(signal, filter_taps, grad_out):
    rows_local, channels = signal.shape
    devices = lax.axis_size("gx") * lax.axis_size("gy")
    tiles = rows_local // LANES
    rows = devices * tiles
    own = channels // devices
    outer, inner, turn = make_tables(rows)
    x = jnp.stack([filter_taps, signal, grad_out])
    x = x.reshape(3, tiles, LANES, channels).transpose(0, 3, 1, 2)
    x = lax.all_to_all(x, ("gx", "gy"), split_axis=1, concat_axis=2, tiled=True)
    vmem = pl.BlockSpec(memory_space=pltpu.VMEM)
    y = pl.pallas_call(
        local_kernel,
        out_shape=jax.ShapeDtypeStruct((2, own, rows, LANES), f32),
        in_specs=[vmem] * 4,
        out_specs=vmem,
        scratch_shapes=[
            pltpu.VMEM((rows, 6 * LANES), bf16),
            pltpu.VMEM((rows, 6 * LANES), bf16),
            pltpu.VMEM((2 * rows, 6 * LANES), f32),
        ],
        compiler_params=pltpu.CompilerParams(vmem_limit_bytes=60 << 20),
    )(x, outer, inner, turn)
    y = lax.all_to_all(y, ("gx", "gy"), split_axis=2, concat_axis=1, tiled=True)
    y = y.transpose(0, 2, 3, 1).reshape(2, rows_local, channels)
    return y[0], y[1]


def solution(mesh):
    spec = P(("gx", "gy"), None)
    return jax.shard_map(
        shards, mesh=mesh, in_specs=(spec,) * 3, out_specs=(spec,) * 2, check_vma=False
    )
```

```python
import functools
import math

import jax
import jax.numpy as jnp
import numpy as np
from jax import lax
from jax.experimental import pallas as pl
from jax.experimental.pallas import tpu as pltpu
from jax.sharding import PartitionSpec as P

LANES = 128
f32, bf16 = jnp.float32, jnp.bfloat16


def halves(table):
    high = table.astype(np.float32).astype(bf16)
    low = (table - high.astype(np.float64)).astype(np.float32).astype(bf16)
    return np.stack([high, low])


def make_tables(rows):
    first = 2 * rows
    period = first * LANES
    low = np.arange(rows)
    angle = 2.0 * math.pi / first * (low[:, None] * low[None, :] % first)
    outer = np.concatenate([np.cos(angle), np.sin(angle)], axis=0)
    lane = np.arange(LANES)
    angle = 2.0 * math.pi / LANES * (lane[:, None] * lane[None, :] % LANES)
    c, s = np.cos(angle), np.sin(angle)
    inner = np.concatenate(
        [np.concatenate([c, s], axis=1), np.concatenate([-s, c], axis=1)], axis=0
    )
    angle = 2.0 * math.pi / period * (np.arange(first)[:, None] * lane[None, :] % period)
    turn = np.stack([np.cos(angle), np.sin(angle)]).astype(np.float32)
    return halves(outer), halves(inner), turn


def split(value):
    high = value.astype(bf16)
    return high, (value - high.astype(f32)).astype(bf16)


def mm(a, b):
    return jnp.dot(a, b, preferred_element_type=f32)


def left_product(outer_ref, high_ref, low_ref, out_ref, width):
    total = outer_ref.shape[1]
    block = min(total, 512)

    def step(rows):
        high = high_ref[:, :width]
        low = low_ref[:, :width]
        out_ref[rows, :width] = (
            mm(outer_ref[0, rows, :], high)
            + mm(outer_ref[0, rows, :], low)
            + mm(outer_ref[1, rows, :], high)
        )

    if block == total:
        step(slice(None))
    else:

        @pl.loop(0, total // block)
        def _(i):
            step(pl.ds(pl.multiple_of(i * block, block), block))


def right_product(value, inner_ref):
    high, low = split(value)
    return mm(high, inner_ref[0]) + mm(low, inner_ref[0]) + mm(high, inner_ref[1])


def correlate(load, store, rows, outer_ref, inner_ref, turn_ref, high_ref, low_ref, prod_ref):
    odd = lax.broadcasted_iota(jnp.int32, (rows, LANES), 0) % 2 == 1
    for q in range(3):
        high, low = split(load(q))
        high32, low32 = high.astype(f32), low.astype(f32)
        at = slice(q * LANES, (q + 1) * LANES)
        high_ref[:, at], low_ref[:, at] = high, low
        at = slice((q + 3) * LANES, (q + 4) * LANES)
        high_ref[:, at] = jnp.where(odd, -high32, high32).astype(bf16)
        low_ref[:, at] = jnp.where(odd, -low32, low32).astype(bf16)
    left_product(outer_ref, high_ref, low_ref, prod_ref, 6 * LANES)
    for h in range(2):

        def part(which, q):
            at = (q + 3 * h) * LANES
            return prod_ref[which * rows : (which + 1) * rows, at : at + LANES]

        cosine = turn_ref[0, h * rows : (h + 1) * rows, :]
        sine = turn_ref[1, h * rows : (h + 1) * rows, :]

        def rotate(real, imaginary):
            return jnp.concatenate(
                [real * cosine - imaginary * sine, real * sine + imaginary * cosine], axis=1
            )

        z = rotate(part(0, 0) - part(1, 1), part(1, 0) + part(0, 1))
        g = rotate(part(0, 2), part(1, 2))
        z = right_product(z, inner_ref)
        g = right_product(g, inner_ref)
        zr, zi, gr, gi = z[:, :LANES], z[:, LANES:], g[:, :LANES], g[:, LANES:]
        y = jnp.concatenate([zr * gr + zi * gi, zi * gr - zr * gi], axis=1)
        y = right_product(y, inner_ref)
        y = rotate(y[:, :LANES], y[:, LANES:])
        high, low = split(y)
        at = slice(2 * h * LANES, 2 * (h + 1) * LANES)
        high_ref[:, at], low_ref[:, at] = high, low
    left_product(outer_ref, high_ref, low_ref, prod_ref, 4 * LANES)
    scale = 1.0 / (2 * rows * LANES)

    def part(which, q):
        return prod_ref[which * rows : (which + 1) * rows, q * LANES : (q + 1) * LANES]

    real = [part(0, 2 * h) - part(1, 2 * h + 1) for h in range(2)]
    imaginary = [part(1, 2 * h) + part(0, 2 * h + 1) for h in range(2)]
    store(0, (real[0] + jnp.where(odd, -real[1], real[1])) * scale)
    store(1, (imaginary[0] + jnp.where(odd, -imaginary[1], imaginary[1])) * scale)


def peer_of(me, offset, devices):
    if devices & (devices - 1):
        return (me + offset) % devices
    peer = me
    bit = 1
    while bit < devices:
        peer = peer + (offset // bit % 2) * (1 - 2 * (me // bit % 2)) * bit
        bit *= 2
    return peer


def kernel(
    columns,
    signal_ref,
    filter_ref,
    grad_ref,
    outer_hbm,
    inner_hbm,
    turn_hbm,
    out0_ref,
    out1_ref,
    send,
    recv,
    back,
    land,
    outer_ref,
    inner_ref,
    turn_ref,
    high_ref,
    low_ref,
    prod_ref,
    table_sem,
    send_sem,
    recv_sem,
    back_sem,
    land_sem,
):
    own, devices, height, _ = recv.shape
    tiles = height // 3
    rows = devices * tiles
    me = lax.axis_index("gx") * columns + lax.axis_index("gy")

    def device(peer):
        return (peer // columns, peer % columns)

    def partner(i):
        return peer_of(me, devices - 1 - i, devices)

    barrier = pltpu.get_barrier_semaphore()

    @pl.loop(0, devices - 1)
    def _(i):
        pl.semaphore_signal(
            barrier, inc=1, device_id=device(partner(i)), device_id_type=pl.DeviceIdType.MESH
        )

    tables = [
        pltpu.make_async_copy(a, b, table_sem.at[n])
        for n, (a, b) in enumerate(
            ((outer_hbm, outer_ref), (inner_hbm, inner_ref), (turn_hbm, turn_ref))
        )
    ]
    for copy in tables:
        copy.start()
    for q, ref in enumerate((filter_ref, signal_ref, grad_ref)):
        for j in range(tiles):
            block = ref[j * LANES : (j + 1) * LANES, :].T
            send[pl.ds(q * tiles + j, own * devices, stride=3 * tiles), :] = block
    pl.semaphore_wait(barrier, devices - 1)

    def outgoing(c, peer):
        at = pl.multiple_of((peer * own + c) * 3 * tiles, 3 * tiles)
        return pltpu.make_async_remote_copy(
            src_ref=send.at[pl.ds(at, 3 * tiles), :],
            dst_ref=recv.at[c, me],
            send_sem=send_sem,
            recv_sem=recv_sem.at[c],
            device_id=device(peer),
            device_id_type=pl.DeviceIdType.MESH,
        )

    def returning(c, peer):
        at = pl.multiple_of((me * own + c) * 2 * tiles, 2 * tiles)
        return pltpu.make_async_remote_copy(
            src_ref=back.at[c, peer],
            dst_ref=land.at[pl.ds(at, 2 * tiles), :],
            send_sem=back_sem,
            recv_sem=land_sem,
            device_id=device(peer),
            device_id_type=pl.DeviceIdType.MESH,
        )

    @pl.loop(0, own)
    def _(c):
        @pl.loop(0, devices - 1)
        def _(i):
            outgoing(c, partner(i)).start()

    @pl.loop(0, own)
    def _(c):
        at = pl.multiple_of((me * own + c) * 3 * tiles, 3 * tiles)
        recv[c, me] = send[pl.ds(at, 3 * tiles), :]

    for copy in tables:
        copy.wait()

    @pl.loop(0, own)
    def _(c):
        arrived = recv.at[c, pl.ds(0, devices - 1)]
        pltpu.make_async_copy(arrived, arrived, recv_sem.at[c]).wait()

        def load(q):
            return recv[c, :, q * tiles : (q + 1) * tiles, :].reshape(rows, LANES)

        def store(q, value):
            back[c, :, q * tiles : (q + 1) * tiles, :] = value.reshape(devices, tiles, LANES)

        correlate(
            load, store, rows, outer_ref, inner_ref, turn_ref, high_ref, low_ref, prod_ref
        )

        @pl.loop(0, devices - 1)
        def _(i):
            returning(c, partner(i)).start()

        at = pl.multiple_of((me * own + c) * 2 * tiles, 2 * tiles)
        land[pl.ds(at, 2 * tiles), :] = back[c, me]

    landed = land.at[pl.ds(0, (devices - 1) * own * 2 * tiles), :]
    pltpu.make_async_copy(landed, landed, land_sem).wait()
    for q, ref in enumerate((out0_ref, out1_ref)):
        for j in range(tiles):
            block = land[pl.ds(q * tiles + j, own * devices, stride=2 * tiles), :]
            ref[j * LANES : (j + 1) * LANES, :] = block.T
    sent = send.at[pl.ds(0, (devices - 1) * own * 3 * tiles), :]
    pltpu.make_async_copy(sent, sent, send_sem).wait()
    pltpu.make_async_copy(landed, landed, back_sem).wait()


def shards(signal, filter_taps, grad_out):
    rows_local, channels = signal.shape
    columns = lax.axis_size("gy")
    devices = lax.axis_size("gx") * columns
    tiles = rows_local // LANES
    rows = devices * tiles
    own = channels // devices
    outer, inner, turn = make_tables(rows)
    vmem = pl.BlockSpec(memory_space=pltpu.VMEM)
    anywhere = pl.BlockSpec(memory_space=pl.ANY)
    result = jax.ShapeDtypeStruct((rows_local, channels), f32)
    return pl.pallas_call(
        functools.partial(kernel, columns),
        out_shape=(result, result),
        in_specs=[vmem] * 3 + [anywhere] * 3,
        out_specs=(vmem, vmem),
        scratch_shapes=[
            pltpu.VMEM((channels * 3 * tiles, LANES), f32),
            pltpu.VMEM((own, devices, 3 * tiles, LANES), f32),
            pltpu.VMEM((own, devices, 2 * tiles, LANES), f32),
            pltpu.VMEM((channels * 2 * tiles, LANES), f32),
            pltpu.VMEM(outer.shape, bf16),
            pltpu.VMEM(inner.shape, bf16),
            pltpu.VMEM(turn.shape, f32),
            pltpu.VMEM((rows, 6 * LANES), bf16),
            pltpu.VMEM((rows, 6 * LANES), bf16),
            pltpu.VMEM((2 * rows, 6 * LANES), f32),
            pltpu.SemaphoreType.DMA((3,)),
            pltpu.SemaphoreType.DMA,
            pltpu.SemaphoreType.DMA((own,)),
            pltpu.SemaphoreType.DMA,
            pltpu.SemaphoreType.DMA,
        ],
        compiler_params=pltpu.CompilerParams(
            collective_id=0, has_side_effects=True, vmem_limit_bytes=60 << 20
        ),
    )(signal, filter_taps, grad_out, outer, inner, turn)


def solution(mesh):
    spec = P(("gx", "gy"), None)
    return jax.shard_map(
        shards, mesh=mesh, in_specs=(spec,) * 3, out_specs=(spec,) * 2, check_vma=False
    )
```

```python
import functools
import math

import jax
import jax.numpy as jnp
import numpy as np
from jax import lax
from jax.experimental import pallas as pl
from jax.experimental.pallas import tpu as pltpu
from jax.sharding import PartitionSpec as P

LANES = 128
f32, bf16 = jnp.float32, jnp.bfloat16


def halves(table):
    high = table.astype(np.float32).astype(bf16)
    low = (table - high.astype(np.float64)).astype(np.float32).astype(bf16)
    return np.stack([high, low])


def make_tables(rows):
    first = 2 * rows
    period = first * LANES
    low = np.arange(rows)
    angle = 2.0 * math.pi / first * (low[:, None] * low[None, :] % first)
    outer = np.concatenate([np.cos(angle), np.sin(angle)], axis=0)
    lane = np.arange(LANES)
    angle = 2.0 * math.pi / LANES * (lane[:, None] * lane[None, :] % LANES)
    c, s = np.cos(angle), np.sin(angle)
    inner = np.concatenate(
        [np.concatenate([c, s], axis=1), np.concatenate([-s, c], axis=1)], axis=0
    )
    angle = 2.0 * math.pi / period * (np.arange(first)[:, None] * lane[None, :] % period)
    turn = np.stack([np.cos(angle), np.sin(angle)]).astype(np.float32)
    return halves(outer), halves(inner), turn


def split(value):
    high = value.astype(bf16)
    return high, (value - high.astype(f32)).astype(bf16)


def mm(a, b):
    return jnp.dot(a, b, preferred_element_type=f32)


def left_product(outer_ref, high_ref, low_ref, out_ref, width):
    total = outer_ref.shape[1]
    block = min(total, 512)

    def step(rows):
        high = high_ref[:, :width]
        low = low_ref[:, :width]
        out_ref[rows, :width] = (
            mm(outer_ref[0, rows, :], high)
            + mm(outer_ref[0, rows, :], low)
            + mm(outer_ref[1, rows, :], high)
        )

    if block == total:
        step(slice(None))
    else:

        @pl.loop(0, total // block)
        def _(i):
            step(pl.ds(pl.multiple_of(i * block, block), block))


def right_product(value, inner_ref):
    high, low = split(value)
    return mm(high, inner_ref[0]) + mm(low, inner_ref[0]) + mm(high, inner_ref[1])


def correlate(load, store, rows, outer_ref, inner_ref, turn_ref, high_ref, low_ref, prod_ref):
    odd = lax.broadcasted_iota(jnp.int32, (rows, LANES), 0) % 2 == 1
    for q in range(3):
        high, low = split(load(q))
        high32, low32 = high.astype(f32), low.astype(f32)
        at = slice(q * LANES, (q + 1) * LANES)
        high_ref[:, at], low_ref[:, at] = high, low
        at = slice((q + 3) * LANES, (q + 4) * LANES)
        high_ref[:, at] = jnp.where(odd, -high32, high32).astype(bf16)
        low_ref[:, at] = jnp.where(odd, -low32, low32).astype(bf16)
    left_product(outer_ref, high_ref, low_ref, prod_ref, 6 * LANES)
    for h in range(2):

        def part(which, q):
            at = (q + 3 * h) * LANES
            return prod_ref[which * rows : (which + 1) * rows, at : at + LANES]

        cosine = turn_ref[0, h * rows : (h + 1) * rows, :]
        sine = turn_ref[1, h * rows : (h + 1) * rows, :]

        def rotate(real, imaginary):
            return jnp.concatenate(
                [real * cosine - imaginary * sine, real * sine + imaginary * cosine], axis=1
            )

        z = rotate(part(0, 0) - part(1, 1), part(1, 0) + part(0, 1))
        g = rotate(part(0, 2), part(1, 2))
        z = right_product(z, inner_ref)
        g = right_product(g, inner_ref)
        zr, zi, gr, gi = z[:, :LANES], z[:, LANES:], g[:, :LANES], g[:, LANES:]
        y = jnp.concatenate([zr * gr + zi * gi, zi * gr - zr * gi], axis=1)
        y = right_product(y, inner_ref)
        y = rotate(y[:, :LANES], y[:, LANES:])
        high, low = split(y)
        at = slice(2 * h * LANES, 2 * (h + 1) * LANES)
        high_ref[:, at], low_ref[:, at] = high, low
    left_product(outer_ref, high_ref, low_ref, prod_ref, 4 * LANES)
    scale = 1.0 / (2 * rows * LANES)

    def part(which, q):
        return prod_ref[which * rows : (which + 1) * rows, q * LANES : (q + 1) * LANES]

    real = [part(0, 2 * h) - part(1, 2 * h + 1) for h in range(2)]
    imaginary = [part(1, 2 * h) + part(0, 2 * h + 1) for h in range(2)]
    store(0, (real[0] + jnp.where(odd, -real[1], real[1])) * scale)
    store(1, (imaginary[0] + jnp.where(odd, -imaginary[1], imaginary[1])) * scale)


def peer_of(me, offset, devices):
    if devices & (devices - 1):
        return (me + offset) % devices
    peer = me
    bit = 1
    while bit < devices:
        peer = peer + (offset // bit % 2) * (1 - 2 * (me // bit % 2)) * bit
        bit *= 2
    return peer


def kernel(
    columns,
    signal_hbm,
    filter_hbm,
    grad_hbm,
    outer_hbm,
    inner_hbm,
    turn_hbm,
    land,
    block_ref,
    send,
    recv,
    back,
    outer_ref,
    inner_ref,
    turn_ref,
    high_ref,
    low_ref,
    prod_ref,
    block_sem,
    table_sem,
    send_sem,
    recv_sem,
    back_sem,
    land_sem,
    own_sem,
):
    own, devices, height, _ = recv.shape
    tiles = height // 3
    rows = devices * tiles
    me = lax.axis_index("gx") * columns + lax.axis_index("gy")

    def device(peer):
        return (peer // columns, peer % columns)

    def partner(i):
        return peer_of(me, i + 1, devices)

    blocks = [
        pltpu.make_async_copy(ref, block_ref.at[q], block_sem.at[q])
        for q, ref in enumerate((filter_hbm, signal_hbm, grad_hbm))
    ]
    for copy in blocks:
        copy.start()
    barrier = pltpu.get_barrier_semaphore()

    @pl.loop(0, devices - 1)
    def _(i):
        pl.semaphore_signal(
            barrier, inc=1, device_id=device(partner(i)), device_id_type=pl.DeviceIdType.MESH
        )

    tables = [
        pltpu.make_async_copy(a, b, table_sem.at[n])
        for n, (a, b) in enumerate(
            ((outer_hbm, outer_ref), (inner_hbm, inner_ref), (turn_hbm, turn_ref))
        )
    ]
    for copy in tables:
        copy.start()
    for q in range(3):
        blocks[q].wait()
        for j in range(tiles):
            block = block_ref[q, j * LANES : (j + 1) * LANES, :].T
            send[pl.ds(q * tiles + j, own * devices, stride=3 * tiles), :] = block
    pl.semaphore_wait(barrier, devices - 1)

    def outgoing(c, peer):
        at = pl.multiple_of((peer * own + c) * 3 * tiles, 3 * tiles)
        return pltpu.make_async_remote_copy(
            src_ref=send.at[pl.ds(at, 3 * tiles), :],
            dst_ref=recv.at[c, me],
            send_sem=send_sem,
            recv_sem=recv_sem.at[c],
            device_id=device(peer),
            device_id_type=pl.DeviceIdType.MESH,
        )

    def returning(c, peer):
        at = pl.multiple_of((me * own + c) * 2 * tiles, 2 * tiles)
        return pltpu.make_async_remote_copy(
            src_ref=back.at[c, peer],
            dst_ref=land.at[pl.ds(at, 2 * tiles), :],
            send_sem=back_sem,
            recv_sem=land_sem,
            device_id=device(peer),
            device_id_type=pl.DeviceIdType.MESH,
        )

    def keep(c):
        at = pl.multiple_of((me * own + c) * 2 * tiles, 2 * tiles)
        return pltpu.make_async_copy(
            back.at[c, me], land.at[pl.ds(at, 2 * tiles), :], own_sem.at[c]
        )

    @pl.loop(0, own)
    def _(c):
        @pl.loop(0, devices - 1)
        def _(i):
            outgoing(c, partner(i)).start()

    @pl.loop(0, own)
    def _(c):
        at = pl.multiple_of((me * own + c) * 3 * tiles, 3 * tiles)
        recv[c, me] = send[pl.ds(at, 3 * tiles), :]

    for copy in tables:
        copy.wait()

    @pl.loop(0, own)
    def _(c):
        arrived = recv.at[c, pl.ds(0, devices - 1)]
        pltpu.make_async_copy(arrived, arrived, recv_sem.at[c]).wait()

        def load(q):
            return recv[c, :, q * tiles : (q + 1) * tiles, :].reshape(rows, LANES)

        def store(q, value):
            back[c, :, q * tiles : (q + 1) * tiles, :] = value.reshape(devices, tiles, LANES)

        correlate(
            load, store, rows, outer_ref, inner_ref, turn_ref, high_ref, low_ref, prod_ref
        )

        @pl.loop(0, devices - 1)
        def _(i):
            returning(c, partner(i)).start()

        keep(c).start()

    landed = land.at[pl.ds(0, (devices - 1) * own * 2 * tiles), :]
    pltpu.make_async_copy(landed, landed, land_sem).wait()

    @pl.loop(0, own)
    def _(c):
        keep(c).wait()

    sent = send.at[pl.ds(0, (devices - 1) * own * 3 * tiles), :]
    pltpu.make_async_copy(sent, sent, send_sem).wait()
    pltpu.make_async_copy(landed, landed, back_sem).wait()


def spread_kernel(land, out0_ref, out1_ref):
    tiles = out0_ref.shape[0] // LANES
    channels = out0_ref.shape[1]
    for q, ref in enumerate((out0_ref, out1_ref)):
        for j in range(tiles):
            block = land[pl.ds(q * tiles + j, channels, stride=2 * tiles), :]
            ref[j * LANES : (j + 1) * LANES, :] = block.T


def shards(signal, filter_taps, grad_out):
    rows_local, channels = signal.shape
    columns = lax.axis_size("gy")
    devices = lax.axis_size("gx") * columns
    tiles = rows_local // LANES
    rows = devices * tiles
    own = channels // devices
    outer, inner, turn = make_tables(rows)
    vmem = pl.BlockSpec(memory_space=pltpu.VMEM)
    anywhere = pl.BlockSpec(memory_space=pl.ANY)
    result = jax.ShapeDtypeStruct((rows_local, channels), f32)
    land = pl.pallas_call(
        functools.partial(kernel, columns),
        out_shape=jax.ShapeDtypeStruct((channels * 2 * tiles, LANES), f32),
        in_specs=[anywhere] * 6,
        out_specs=anywhere,
        scratch_shapes=[
            pltpu.VMEM((3, rows_local, channels), f32),
            pltpu.VMEM((channels * 3 * tiles, LANES), f32),
            pltpu.VMEM((own, devices, 3 * tiles, LANES), f32),
            pltpu.VMEM((own, devices, 2 * tiles, LANES), f32),
            pltpu.VMEM(outer.shape, bf16),
            pltpu.VMEM(inner.shape, bf16),
            pltpu.VMEM(turn.shape, f32),
            pltpu.VMEM((rows, 6 * LANES), bf16),
            pltpu.VMEM((rows, 6 * LANES), bf16),
            pltpu.VMEM((2 * rows, 6 * LANES), f32),
            pltpu.SemaphoreType.DMA((3,)),
            pltpu.SemaphoreType.DMA((3,)),
            pltpu.SemaphoreType.DMA,
            pltpu.SemaphoreType.DMA((own,)),
            pltpu.SemaphoreType.DMA,
            pltpu.SemaphoreType.DMA,
            pltpu.SemaphoreType.DMA((own,)),
        ],
        compiler_params=pltpu.CompilerParams(
            collective_id=0, has_side_effects=True, vmem_limit_bytes=60 << 20
        ),
    )(signal, filter_taps, grad_out, outer, inner, turn)
    return pl.pallas_call(
        spread_kernel,
        out_shape=(result, result),
        in_specs=[vmem],
        out_specs=(vmem, vmem),
        compiler_params=pltpu.CompilerParams(vmem_limit_bytes=60 << 20),
    )(land)


def solution(mesh):
    spec = P(("gx", "gy"), None)
    return jax.shard_map(
        shards, mesh=mesh, in_specs=(spec,) * 3, out_specs=(spec,) * 2, check_vma=False
    )
```

```python
import functools
import math

import jax
import jax.numpy as jnp
import numpy as np
from jax import lax
from jax.experimental import pallas as pl
from jax.experimental.pallas import tpu as pltpu
from jax.sharding import PartitionSpec as P

LANES = 128
f32, bf16 = jnp.float32, jnp.bfloat16


def halves(table):
    high = table.astype(np.float32).astype(bf16)
    low = (table - high.astype(np.float64)).astype(np.float32).astype(bf16)
    return np.stack([high, low])


def make_tables(rows):
    first = 2 * rows
    period = first * LANES
    low = np.arange(rows)
    angle = 2.0 * math.pi / first * (low[:, None] * low[None, :] % first)
    outer = np.concatenate([np.cos(angle), np.sin(angle)], axis=0)
    lane = np.arange(LANES)
    angle = 2.0 * math.pi / LANES * (lane[:, None] * lane[None, :] % LANES)
    c, s = np.cos(angle), np.sin(angle)
    inner = np.concatenate(
        [np.concatenate([c, s], axis=1), np.concatenate([-s, c], axis=1)], axis=0
    )
    angle = 2.0 * math.pi / period * (np.arange(first)[:, None] * lane[None, :] % period)
    turn = np.stack([np.cos(angle), np.sin(angle)]).astype(np.float32)
    return halves(outer), halves(inner), turn


def split(value):
    high = value.astype(bf16)
    return high, (value - high.astype(f32)).astype(bf16)


def mm(a, b):
    return jnp.dot(a, b, preferred_element_type=f32)


def left_product(outer_ref, high_ref, low_ref, out_ref, width):
    total = outer_ref.shape[1]
    block = min(total, 512)

    def step(rows):
        high = high_ref[:, :width]
        low = low_ref[:, :width]
        out_ref[rows, :width] = (
            mm(outer_ref[0, rows, :], high)
            + mm(outer_ref[0, rows, :], low)
            + mm(outer_ref[1, rows, :], high)
        )

    if block == total:
        step(slice(None))
    else:

        @pl.loop(0, total // block)
        def _(i):
            step(pl.ds(pl.multiple_of(i * block, block), block))


def right_product(value, inner_ref):
    high, low = split(value)
    return mm(high, inner_ref[0]) + mm(low, inner_ref[0]) + mm(high, inner_ref[1])


def correlate(load, store, rows, outer_ref, inner_ref, turn_ref, high_ref, low_ref, prod_ref):
    odd = lax.broadcasted_iota(jnp.int32, (rows, LANES), 0) % 2 == 1
    for q in range(3):
        high, low = split(load(q))
        high32, low32 = high.astype(f32), low.astype(f32)
        at = slice(q * LANES, (q + 1) * LANES)
        high_ref[:, at], low_ref[:, at] = high, low
        at = slice((q + 3) * LANES, (q + 4) * LANES)
        high_ref[:, at] = jnp.where(odd, -high32, high32).astype(bf16)
        low_ref[:, at] = jnp.where(odd, -low32, low32).astype(bf16)
    left_product(outer_ref, high_ref, low_ref, prod_ref, 6 * LANES)
    for h in range(2):

        def part(which, q):
            at = (q + 3 * h) * LANES
            return prod_ref[which * rows : (which + 1) * rows, at : at + LANES]

        cosine = turn_ref[0, h * rows : (h + 1) * rows, :]
        sine = turn_ref[1, h * rows : (h + 1) * rows, :]

        def rotate(real, imaginary):
            return jnp.concatenate(
                [real * cosine - imaginary * sine, real * sine + imaginary * cosine], axis=1
            )

        z = rotate(part(0, 0) - part(1, 1), part(1, 0) + part(0, 1))
        g = rotate(part(0, 2), part(1, 2))
        z = right_product(z, inner_ref)
        g = right_product(g, inner_ref)
        zr, zi, gr, gi = z[:, :LANES], z[:, LANES:], g[:, :LANES], g[:, LANES:]
        y = jnp.concatenate([zr * gr + zi * gi, zi * gr - zr * gi], axis=1)
        y = right_product(y, inner_ref)
        y = rotate(y[:, :LANES], y[:, LANES:])
        high, low = split(y)
        at = slice(2 * h * LANES, 2 * (h + 1) * LANES)
        high_ref[:, at], low_ref[:, at] = high, low
    left_product(outer_ref, high_ref, low_ref, prod_ref, 4 * LANES)
    scale = 1.0 / (2 * rows * LANES)

    def part(which, q):
        return prod_ref[which * rows : (which + 1) * rows, q * LANES : (q + 1) * LANES]

    real = [part(0, 2 * h) - part(1, 2 * h + 1) for h in range(2)]
    imaginary = [part(1, 2 * h) + part(0, 2 * h + 1) for h in range(2)]
    store(0, (real[0] + jnp.where(odd, -real[1], real[1])) * scale)
    store(1, (imaginary[0] + jnp.where(odd, -imaginary[1], imaginary[1])) * scale)


def peer_of(me, offset, devices):
    if devices & (devices - 1):
        return (me + offset) % devices
    peer = me
    bit = 1
    while bit < devices:
        peer = peer + (offset // bit % 2) * (1 - 2 * (me // bit % 2)) * bit
        bit *= 2
    return peer


def kernel(
    columns,
    signal_hbm,
    filter_hbm,
    grad_hbm,
    outer_hbm,
    inner_hbm,
    turn_hbm,
    land,
    block_ref,
    send,
    recv,
    back,
    outer_ref,
    inner_ref,
    turn_ref,
    high_ref,
    low_ref,
    prod_ref,
    block_sem,
    table_sem,
    send_sem,
    recv_sem,
    back_sem,
    land_sem,
    own_sem,
):
    own, devices, height, _ = recv.shape
    tiles = height // 3
    rows = devices * tiles
    me = lax.axis_index("gx") * columns + lax.axis_index("gy")

    def device(peer):
        return (peer // columns, peer % columns)

    def partner(i):
        return peer_of(me, i + 1, devices)

    blocks = [
        pltpu.make_async_copy(ref, block_ref.at[q], block_sem.at[q])
        for q, ref in enumerate((filter_hbm, signal_hbm, grad_hbm))
    ]
    for copy in blocks:
        copy.start()
    barrier = pltpu.get_barrier_semaphore()

    @pl.loop(0, devices - 1)
    def _(i):
        pl.semaphore_signal(
            barrier,
            inc=1,
            device_id=device(partner(devices - 2 - i)),
            device_id_type=pl.DeviceIdType.MESH,
        )

    tables = [
        pltpu.make_async_copy(a, b, table_sem.at[n])
        for n, (a, b) in enumerate(
            ((outer_hbm, outer_ref), (inner_hbm, inner_ref), (turn_hbm, turn_ref))
        )
    ]
    for copy in tables:
        copy.start()
    def turn_block(q):
        blocks[q].wait()
        for j in range(tiles):
            block = block_ref[q, j * LANES : (j + 1) * LANES, :].T
            send[pl.ds(q * tiles + j, own * devices, stride=3 * tiles), :] = block
    def outgoing(c, peer, begin, end):
        at = pl.multiple_of((peer * own + c) * 3 * tiles + begin * tiles, tiles)
        return pltpu.make_async_remote_copy(
            src_ref=send.at[pl.ds(at, (end - begin) * tiles), :],
            dst_ref=recv.at[c, me, begin * tiles : end * tiles, :],
            send_sem=send_sem,
            recv_sem=recv_sem.at[c],
            device_id=device(peer),
            device_id_type=pl.DeviceIdType.MESH,
        )

    def returning(c, peer):
        at = pl.multiple_of((me * own + c) * tiles, tiles)
        return pltpu.make_async_remote_copy(
            src_ref=back.at[c, peer],
            dst_ref=land.at[:, pl.ds(at, tiles), :],
            send_sem=back_sem,
            recv_sem=land_sem,
            device_id=device(peer),
            device_id_type=pl.DeviceIdType.MESH,
        )

    def keep(c):
        at = pl.multiple_of((me * own + c) * tiles, tiles)
        return pltpu.make_async_copy(
            back.at[c, me], land.at[:, pl.ds(at, tiles), :], own_sem.at[c]
        )

    turn_block(0)
    pl.semaphore_wait(barrier, devices - 1)

    @pl.loop(0, devices - 1)
    def _(i):
        outgoing(0, partner(i), 0, 1).start()

    turn_block(1)
    turn_block(2)

    @pl.loop(0, devices - 1)
    def _(i):
        outgoing(0, partner(i), 1, 3).start()

    @pl.loop(1, own)
    def _(c):
        @pl.loop(0, devices - 1)
        def _(i):
            outgoing(c, partner(i), 0, 3).start()

    @pl.loop(0, own)
    def _(c):
        at = pl.multiple_of((me * own + c) * 3 * tiles, 3 * tiles)
        recv[c, me] = send[pl.ds(at, 3 * tiles), :]

    for copy in tables:
        copy.wait()

    @pl.loop(0, own)
    def _(c):
        arrived = recv.at[c, pl.ds(0, devices - 1)]
        pltpu.make_async_copy(arrived, arrived, recv_sem.at[c]).wait()

        def load(q):
            return recv[c, :, q * tiles : (q + 1) * tiles, :].reshape(rows, LANES)

        def store(q, value):
            back[c, :, q] = value.reshape(devices, tiles, LANES)

        correlate(
            load, store, rows, outer_ref, inner_ref, turn_ref, high_ref, low_ref, prod_ref
        )

        @pl.loop(0, devices - 1)
        def _(i):
            returning(c, partner(i)).start()

        keep(c).start()

    landed = land.at[:, pl.ds(0, (devices - 1) * own * tiles), :]
    pltpu.make_async_copy(landed, landed, land_sem).wait()

    @pl.loop(0, own)
    def _(c):
        keep(c).wait()

    sent = send.at[pl.ds(0, (devices - 1) * own * 3 * tiles), :]
    pltpu.make_async_copy(sent, sent, send_sem).wait()
    pltpu.make_async_copy(landed, landed, back_sem).wait()


def spread_kernel(land, out0_ref, out1_ref, land_ref, result_ref, in_sem, out_sem):
    _, rows_local, channels = result_ref.shape
    tiles = rows_local // LANES
    reads = [
        pltpu.make_async_copy(land.at[q], land_ref.at[q], in_sem.at[q]) for q in range(2)
    ]
    for copy in reads:
        copy.start()
    writes = []
    half = rows_local // 2
    for q, ref in enumerate((out0_ref, out1_ref)):
        reads[q].wait()
        for j in range(tiles):
            block = land_ref[q, pl.ds(j, channels, stride=tiles), :]
            result_ref[q, j * LANES : (j + 1) * LANES, :] = block.T
            if (j + 1) % (tiles // 2) == 0:
                at = slice((j + 1) * LANES - half, (j + 1) * LANES)
                writes.append(
                    pltpu.make_async_copy(
                        result_ref.at[q, at, :], ref.at[at, :], out_sem.at[len(writes)]
                    )
                )
                writes[-1].start()
    for copy in writes:
        copy.wait()


def shards(signal, filter_taps, grad_out):
    rows_local, channels = signal.shape
    columns = lax.axis_size("gy")
    devices = lax.axis_size("gx") * columns
    tiles = rows_local // LANES
    rows = devices * tiles
    own = channels // devices
    outer, inner, turn = make_tables(rows)
    anywhere = pl.BlockSpec(memory_space=pl.ANY)
    result = jax.ShapeDtypeStruct((rows_local, channels), f32)
    land = pl.pallas_call(
        functools.partial(kernel, columns),
        out_shape=jax.ShapeDtypeStruct((2, channels * tiles, LANES), f32),
        in_specs=[anywhere] * 6,
        out_specs=anywhere,
        scratch_shapes=[
            pltpu.VMEM((3, rows_local, channels), f32),
            pltpu.VMEM((channels * 3 * tiles, LANES), f32),
            pltpu.VMEM((own, devices, 3 * tiles, LANES), f32),
            pltpu.VMEM((own, devices, 2, tiles, LANES), f32),
            pltpu.VMEM(outer.shape, bf16),
            pltpu.VMEM(inner.shape, bf16),
            pltpu.VMEM(turn.shape, f32),
            pltpu.VMEM((rows, 6 * LANES), bf16),
            pltpu.VMEM((rows, 6 * LANES), bf16),
            pltpu.VMEM((2 * rows, 6 * LANES), f32),
            pltpu.SemaphoreType.DMA((3,)),
            pltpu.SemaphoreType.DMA((3,)),
            pltpu.SemaphoreType.DMA,
            pltpu.SemaphoreType.DMA((own,)),
            pltpu.SemaphoreType.DMA,
            pltpu.SemaphoreType.DMA,
            pltpu.SemaphoreType.DMA((own,)),
        ],
        compiler_params=pltpu.CompilerParams(
            collective_id=0, has_side_effects=True, vmem_limit_bytes=60 << 20
        ),
    )(signal, filter_taps, grad_out, outer, inner, turn)
    return pl.pallas_call(
        spread_kernel,
        out_shape=(result, result),
        in_specs=[anywhere],
        out_specs=(anywhere, anywhere),
        scratch_shapes=[
            pltpu.VMEM((2, channels * tiles, LANES), f32),
            pltpu.VMEM((2, rows_local, channels), f32),
            pltpu.SemaphoreType.DMA((2,)),
            pltpu.SemaphoreType.DMA((4,)),
        ],
        compiler_params=pltpu.CompilerParams(vmem_limit_bytes=60 << 20),
    )(land)


def solution(mesh):
    spec = P(("gx", "gy"), None)
    return jax.shard_map(
        shards, mesh=mesh, in_specs=(spec,) * 3, out_specs=(spec,) * 2, check_vma=False
    )
```
